32 devices in a mesh: stretch: 2 (over core), seq: 16 (over z, y, x).
Axes of the slice: x: 2, y: 2, z: 4, core: 2. Of those that a mesh axis runs over, the one named last changes fastest.
Arguments:
- queries: bfloat16 [4096, 1024], P(('stretch', 'seq')), may hold values from -16 to 16
- keys: bfloat16 [4096, 1024], P(('stretch', 'seq')), may hold values from -16 to 16
- values: bfloat16 [4096, 1024], P(('stretch', 'seq')), may hold values from -6 to 6
- tokens: bfloat16 [4096, 1536], P(('stretch', 'seq')), may hold values from -6 to 6
- out_weight: bfloat16 [1024, 1536], replicated, may hold values from -0.1875 to 0.1875
- gate_table: float32 [4, 1536], replicated, may hold values from 0.5 to 2
- timesteps: int32 [32], P(('stretch', 'seq')), may hold values from 0 to 3
Outputs:
- mixed: bfloat16 [4096, 1536], P(('stretch', 'seq'))
The draws below stay inside these ranges and needn't reach their ends.
All inputs are finite; a program needn't handle non-finite values.
Results may differ from the reference program's by a relative error of at most 0.0051.
Values may be sent and summed in bfloat16 or wider, within the bound.
A program may use at most 128 MiB of HBM per device.

```python
import math
import jax
import jax.numpy as jnp
from jax import lax

D = 1536
HD = 128
HEADS = 8
SPAN = 3
STEPS = 4
TOK_DEV = 128
TOKENS = 4096
N_STRETCH = 2
N_SEQ = 16


def draw_queries(key, part):
    result = jnp.clip(jax.random.normal(jax.random.fold_in(key, 31), (TOKENS, HEADS * HD), jnp.float32), -4.0, 4.0)
    return result.astype(jnp.bfloat16)


def draw_keys(key, part):
    result = jnp.clip(jax.random.normal(jax.random.fold_in(key, 51), (TOKENS, HEADS * HD), jnp.float32), -4.0, 4.0)
    return result.astype(jnp.bfloat16)


def with_ends(array, own_key, least, high):
    extent = array.shape
    place = [jax.random.randint(jax.random.fold_in(own_key, axis), (), 0, extent[axis]) for axis in range(len(extent))]
    array = array.at[tuple(place)].set(least)
    longest = extent.index(max(extent))
    place[longest] = (place[longest] + 1) % extent[longest]
    return array.at[tuple(place)].set(high)


def level_of(key, extent, split, smallest, top_value):
    def one(dim, parts):
        draws = jax.random.uniform(jax.random.fold_in(jax.random.fold_in(key, 6), dim), (parts,), jnp.float32, smallest / len(split), top_value / len(split))
        return jnp.repeat(jnp.exp(draws), extent[dim] // parts).reshape((-1,) + (1,) * (len(extent) - dim - 1))

    loudness = one(*split[0])
    for cut in split[1:]:
        loudness = loudness * one(*cut)
    return loudness


def scatter_about(key, dims, width, reach, split=(), kind=jnp.bfloat16):
    factor_of = level_of(key, dims, split, -0.22, 0.18) if split else 1.0
    array = jax.random.normal(key, dims, jnp.float32) * width * factor_of
    return jnp.minimum(jnp.maximum(array, -reach), reach).astype(kind)


def setup_inputs(seed: int = 0) -> dict:
    seeds = jax.random.split(jax.random.key(seed), 8)
    return {
        "queries": draw_queries(jax.random.fold_in(seeds[7], 71), 0),
        "keys": draw_keys(jax.random.fold_in(seeds[7], 71), 0),
        "values": scatter_about(seeds[2], (TOKENS, HEADS * HD), 1.0, 6.0, ((0, 32),)),
        "tokens": scatter_about(seeds[3], (TOKENS, D), 1.0, 6.0, ((0, 32),)),
        "out_weight": scatter_about(seeds[4], (HEADS * HD, D), (HEADS * HD) ** -0.5, 0.1875),
        "gate_table": jnp.clip(jnp.exp(jax.random.uniform(seeds[5], (STEPS, D), jnp.float32, math.log(0.5), math.log(2.0))), 0.5, 2.0),
        "timesteps": with_ends(jax.random.randint(seeds[6], (TOKENS // TOK_DEV,), 0, STEPS), jax.random.fold_in(seeds[6], 1), 0, STEPS - 1).astype(jnp.int32),
    }


def reference(queries, keys, values, tokens, out_weight, gate_table, timesteps):
    stretch_tok = TOK_DEV * N_SEQ
    scale = 1.0 / math.sqrt(HD)
    pieces = []
    for stretch in range(N_STRETCH):
        first = max(0, stretch - SPAN + 1)
        query_part = queries[stretch * stretch_tok:(stretch + 1) * stretch_tok].reshape(stretch_tok, HEADS, HD).transpose(1, 0, 2)
        key_part = keys[first * stretch_tok:(stretch + 1) * stretch_tok].reshape(-1, HEADS, HD).transpose(1, 0, 2)
        value_part = values[first * stretch_tok:(stretch + 1) * stretch_tok].reshape(-1, HEADS, HD).transpose(1, 0, 2)

        def one_head(operands):
            query_head, key_head, value_head = operands
            scores = jnp.dot(query_head, key_head.T, preferred_element_type=jnp.float32) * scale
            top = lax.optimization_barrier(jnp.max(scores, axis=1, keepdims=True))
            expo = jnp.exp(scores - top)
            total = lax.optimization_barrier(jnp.sum(expo, axis=1, keepdims=True))
            result = jnp.dot(expo.astype(jnp.bfloat16), value_head, preferred_element_type=jnp.float32)
            return (result / total).astype(jnp.bfloat16)
        attended = lax.map(one_head, (query_part, key_part, value_part))
        attended = attended.transpose(1, 0, 2).reshape(stretch_tok, HEADS * HD)
        proj = jnp.dot(attended, out_weight, preferred_element_type=jnp.float32)
        mean_sq = lax.optimization_barrier(jnp.mean(proj * proj, axis=1, keepdims=True))
        normed = proj * lax.rsqrt(mean_sq + 1e-06)
        block_steps = timesteps[stretch * N_SEQ:(stretch + 1) * N_SEQ]
        gate_rows = jnp.repeat(gate_table[block_steps], TOK_DEV, axis=0)
        resid = tokens[stretch * stretch_tok:(stretch + 1) * stretch_tok].astype(jnp.float32)
        pieces.append((resid + gate_rows * normed).astype(jnp.bfloat16))
    return jnp.concatenate(pieces, axis=0)
```

```python
import functools
import math

import jax
import jax.numpy as jnp
from jax import lax
from jax.experimental import pallas as pl
from jax.experimental.pallas import tpu as pltpu
from jax.sharding import PartitionSpec as P

HD = 128
HEADS = 8
SPAN = 3
MESH = pl.DeviceIdType.MESH


def kernel(groups, stretches, chunk, q_ref, k_ref, v_ref, tok_ref, w_ref, gate_ref, step_ref, out_ref,
           qbuf, kbuf, vbuf, kprior, vprior, top_s, sum_s, acc_s, obuf, att, w_s, tok_s,
           load_sem, local_sem, q_send, q_recv, kv_send, k_recv, v_recv,
           fwd_send, kp_recv, vp_recv, o_send, o_recv):
    count = q_ref.shape[0]
    prior = min(SPAN, stretches) - 1
    chunks = groups // chunk
    stretch = lax.axis_index("stretch")
    me = lax.axis_index("seq")
    head = lax.rem(me, HEADS)
    share = me // HEADS

    def cols(index):
        return pl.ds(pl.multiple_of(index * HD, HD), HD)

    w_copy = pltpu.make_async_copy(w_ref, w_s, load_sem.at[0])
    tok_copy = pltpu.make_async_copy(tok_ref, tok_s, load_sem.at[1])
    own = [
        pltpu.make_async_copy(q_ref.at[:, cols(head)], qbuf.at[head], local_sem.at[0]),
        pltpu.make_async_copy(k_ref.at[:, cols(head)], kbuf.at[me], local_sem.at[1]),
        pltpu.make_async_copy(v_ref.at[:, cols(head)], vbuf.at[me], local_sem.at[2]),
    ]

    barrier = pltpu.get_barrier_semaphore()

    @pl.loop(1, groups)
    def _(off):
        peer = lax.rem(me + off, groups)
        pl.semaphore_signal(barrier, inc=1, device_id=(stretch, peer), device_id_type=MESH)

    for dist in range(1, prior + 1):
        @pl.when(stretch + dist < stretches)
        def _():
            pl.semaphore_signal(barrier, inc=1, device_id=(stretch + dist, me), device_id_type=MESH)

        @pl.when(stretch >= dist)
        def _():
            pl.semaphore_signal(barrier, inc=1, device_id=(stretch - dist, me), device_id_type=MESH)

    for copy in own:
        copy.start()
    w_copy.start()
    tok_copy.start()
    partners = jnp.minimum(stretch, prior) + jnp.minimum(stretches - 1 - stretch, prior)
    pl.semaphore_wait(barrier, groups - 1 + partners)

    def q_copy(off):
        other = lax.rem(head + off, HEADS)
        return pltpu.make_async_remote_copy(
            src_ref=q_ref.at[:, cols(other)], dst_ref=qbuf.at[head],
            send_sem=q_send.at[other], recv_sem=q_recv.at[head],
            device_id=(stretch, share * HEADS + other), device_id_type=MESH)

    def kv_copy(index, which):
        off = 1 + lax.rem(groups // 2 - 1 + index, groups - 1)
        peer = lax.rem(me + off, groups)
        src, dst, recv = ((k_ref, kbuf, k_recv), (v_ref, vbuf, v_recv))[which]
        return pltpu.make_async_remote_copy(
            src_ref=src.at[:, cols(lax.rem(peer, HEADS))], dst_ref=dst.at[me],
            send_sem=kv_send.at[which, peer], recv_sem=recv.at[me],
            device_id=(stretch, peer), device_id_type=MESH)

    @pl.loop(1, HEADS)
    def _(off):
        q_copy(off).start()

    @pl.loop(0, groups - 1)
    def _(index):
        kv_copy(index, 0).start()
        kv_copy(index, 1).start()

    top_s[...] = jnp.full_like(top_s, -1e30)
    sum_s[...] = jnp.zeros_like(sum_s)
    acc_s[...] = jnp.zeros_like(acc_s)

    for copy in own:
        copy.wait()

    def arrived(buf, sems, slot, sends):
        return pltpu.make_async_remote_copy(
            src_ref=buf.at[slot], dst_ref=buf.at[slot], send_sem=sends, recv_sem=sems.at[slot],
            device_id=(stretch, lax.rem(me + 1, groups)), device_id_type=MESH)

    @pl.loop(1, HEADS)
    def _(off):
        arrived(qbuf, q_recv, lax.rem(head + off, HEADS), q_send.at[0]).wait_recv()

    factor = math.log2(math.e) / math.sqrt(HD)
    keys_each = chunk * count
    per = 2 if HEADS % 2 == 0 else 1
    rows = per * count

    def absorb(key_ref, value_ref):
        key_block = key_ref[...].reshape(keys_each, HD)
        value_block = value_ref[...].reshape(keys_each, HD)
        for block in range(HEADS // per):
            span = pl.ds(block * rows, rows)
            query = qbuf[pl.ds(block * per, per)].reshape(rows, HD)
            scores = lax.dot_general(query, key_block, (((1,), (1,)), ((), ())),
                                     preferred_element_type=jnp.float32)
            old = top_s[span, :]
            new = jnp.maximum(old, jnp.max(scores, axis=1, keepdims=True))
            top_s[span, :] = new
            fade = jnp.exp2((old - new) * factor)
            weights = [
                jnp.exp2((scores[:, part * HD:(part + 1) * HD] - new) * factor)
                for part in range(keys_each // HD)
            ]
            sum_s[span, :] = sum_s[span, :] * fade + functools.reduce(jnp.add, weights)
            expo = jnp.concatenate([part.astype(jnp.bfloat16) for part in weights], axis=1)
            acc_s[span, :] = acc_s[span, :] * fade + jnp.dot(
                expo, value_block, preferred_element_type=jnp.float32)

    def forward(first, slot, dist, which):
        src, dst, recv = ((kbuf, kprior, kp_recv), (vbuf, vprior, vp_recv))[which]
        return pltpu.make_async_remote_copy(
            src_ref=src.at[pl.ds(first, chunk)], dst_ref=dst.at[dist - 1, pl.ds(first, chunk)],
            send_sem=fwd_send.at[which, dist - 1, slot], recv_sem=recv.at[dist - 1, slot],
            device_id=(stretch + dist, me), device_id_type=MESH)

    my_chunk = me // chunk
    low = my_chunk < chunks // 2

    def chunk_at(index):
        rising = lax.rem(my_chunk + index, chunks)
        falling = lax.rem(my_chunk + chunks - index, chunks)
        return jnp.where(low, rising, falling)

    @pl.loop(0, chunks)
    def _(index):
        slot = chunk_at(index)
        first = slot * chunk
        for step in range(chunk):
            source = first + step

            @pl.when(source != me)
            def _():
                arrived(kbuf, k_recv, source, kv_send.at[0, 0]).wait_recv()
                arrived(vbuf, v_recv, source, kv_send.at[0, 0]).wait_recv()

        for dist in range(1, prior + 1):
            @pl.when(stretch + dist < stretches)
            def _():
                forward(first, slot, dist, 0).start()
                forward(first, slot, dist, 1).start()

        absorb(kbuf.at[pl.ds(first, chunk)], vbuf.at[pl.ds(first, chunk)])
        for dist in range(1, prior + 1):
            @pl.when(stretch >= dist)
            def _():
                for which in range(2):
                    src, recv = ((kprior, kp_recv), (vprior, vp_recv))[which]
                    pltpu.make_async_remote_copy(
                        src_ref=src.at[dist - 1, pl.ds(first, chunk)],
                        dst_ref=src.at[dist - 1, pl.ds(first, chunk)],
                        send_sem=fwd_send.at[which, dist - 1, slot], recv_sem=recv.at[dist - 1, slot],
                        device_id=(stretch - dist, me), device_id_type=MESH).wait_recv()
                absorb(kprior.at[dist - 1, pl.ds(first, chunk)], vprior.at[dist - 1, pl.ds(first, chunk)])

    for source in range(HEADS):
        span = pl.ds(source * count, count)
        total = jnp.sum(sum_s[span, :], axis=1, keepdims=True)
        obuf[source] = (acc_s[span, :] / total).astype(jnp.bfloat16)

    def o_copy(off):
        other = lax.rem(head + off, HEADS)
        return pltpu.make_async_remote_copy(
            src_ref=obuf.at[other], dst_ref=att.at[:, cols(head)],
            send_sem=o_send.at[other], recv_sem=o_recv.at[head],
            device_id=(stretch, share * HEADS + other), device_id_type=MESH)

    @pl.loop(1, HEADS)
    def _(off):
        o_copy(off).start()

    own_out = pltpu.make_async_copy(obuf.at[head], att.at[:, cols(head)], local_sem.at[0])
    own_out.start()
    w_copy.wait()
    tok_copy.wait()

    table = gate_ref[...]
    picked = lax.broadcasted_iota(jnp.int32, table.shape, 0) == step_ref[0]
    gate = jnp.sum(jnp.where(picked, table, 0.0), axis=0, keepdims=True)

    own_out.wait()

    @pl.loop(1, HEADS)
    def _(off):
        other = lax.rem(head + off, HEADS)
        pltpu.make_async_remote_copy(
            src_ref=obuf.at[other], dst_ref=att.at[:, cols(other)],
            send_sem=o_send.at[other], recv_sem=o_recv.at[other],
            device_id=(stretch, share * HEADS + other), device_id_type=MESH).wait_recv()

    proj = jnp.dot(att[...], w_s[...], preferred_element_type=jnp.float32)
    mean_sq = jnp.mean(proj * proj, axis=1, keepdims=True)
    normed = proj * lax.rsqrt(mean_sq + 1e-06)
    out_ref[...] = (tok_s[...].astype(jnp.float32) + gate * normed).astype(jnp.bfloat16)

    @pl.loop(1, HEADS)
    def _(off):
        q_copy(off).wait_send()
        o_copy(off).wait_send()

    @pl.loop(0, groups - 1)
    def _(index):
        kv_copy(index, 0).wait_send()
        kv_copy(index, 1).wait_send()

    for dist in range(1, prior + 1):
        @pl.when(stretch + dist < stretches)
        def _():
            @pl.loop(0, chunks)
            def _(slot):
                forward(slot * chunk, slot, dist, 0).wait_send()
                forward(slot * chunk, slot, dist, 1).wait_send()


def solution(mesh):
    stretches, groups = mesh.shape["stretch"], mesh.shape["seq"]
    prior = max(1, min(SPAN, stretches) - 1)
    chunk = math.gcd(groups, 4)

    def on_device(queries, keys, values, tokens, out_weight, gate_table, timesteps):
        count = queries.shape[0]
        block = (count, HD)
        dma = pltpu.SemaphoreType.DMA
        anywhere = pl.BlockSpec(memory_space=pl.ANY)
        vmem = pl.BlockSpec(memory_space=pltpu.VMEM)
        rows = HEADS * count
        return pl.pallas_call(
            functools.partial(kernel, groups, stretches, chunk),
            out_shape=jax.ShapeDtypeStruct(tokens.shape, jnp.bfloat16),
            in_specs=[anywhere] * 5 + [vmem, pl.BlockSpec(memory_space=pltpu.SMEM)],
            out_specs=vmem,
            scratch_shapes=[
                pltpu.VMEM((HEADS, *block), jnp.bfloat16),
                pltpu.VMEM((groups, *block), jnp.bfloat16),
                pltpu.VMEM((groups, *block), jnp.bfloat16),
                pltpu.VMEM((prior, groups, *block), jnp.bfloat16),
                pltpu.VMEM((prior, groups, *block), jnp.bfloat16),
                pltpu.VMEM((rows, HD), jnp.float32),
                pltpu.VMEM((rows, HD), jnp.float32),
                pltpu.VMEM((rows, HD), jnp.float32),
                pltpu.VMEM((HEADS, *block), jnp.bfloat16),
                pltpu.VMEM((count, HEADS * HD), jnp.bfloat16),
                pltpu.VMEM(out_weight.shape, jnp.bfloat16),
                pltpu.VMEM(tokens.shape, jnp.bfloat16),
                dma((2,)),
                dma((3,)),
                dma((HEADS,)),
                dma((HEADS,)),
                dma((2, groups)),
                dma((groups,)),
                dma((groups,)),
                dma((2, prior, groups // chunk)),
                dma((prior, groups // chunk)),
                dma((prior, groups // chunk)),
                dma((HEADS,)),
                dma((HEADS,)),
            ],
            compiler_params=pltpu.CompilerParams(collective_id=0, has_side_effects=True),
        )(queries, keys, values, tokens, out_weight, gate_table, timesteps)

    row = P(("stretch", "seq"), None)
    return jax.shard_map(
        on_device, mesh=mesh,
        in_specs=(row, row, row, row, P(), P(), P(("stretch", "seq"))),
        out_specs=row, check_vma=False)
```

```python
import functools
import math

import jax
import jax.numpy as jnp
from jax import lax
from jax.experimental import pallas as pl
from jax.experimental.pallas import tpu as pltpu
from jax.sharding import PartitionSpec as P

HD = 128
HEADS = 8
SPAN = 3
MESH = pl.DeviceIdType.MESH


def flip(base, mask):
    result = base
    for bit in range(mask.bit_length()):
        step = 1 << bit
        if mask & step:
            result = result + step * (1 - 2 * lax.rem(lax.div(base, step), 2))
    return result


def rounds_of(bits):
    known = {0} | {1 << bit for bit in range(bits)}
    rounds = [sorted(known - {0}, reverse=True)]
    for bit in range(bits):
        fresh = {mask ^ (1 << bit) for mask in known} - known
        if not fresh:
            break
        rounds.append(sorted(fresh, reverse=True))
        known |= fresh
    return rounds


def kernel(groups, stretches, chunk, q_ref, k_ref, v_ref, tok_ref, w_ref, gate_ref, step_ref, out_ref,
           qbuf, kbuf, vbuf, kprior, vprior, top_s, sum_s, acc_s, obuf, att, w_s, tok_s,
           load_sem, local_sem, q_send, q_recv, kv_send, k_recv, v_recv,
           fwd_send, kp_recv, vp_recv, o_send, o_recv, ready):
    count = q_ref.shape[0]
    prior = min(SPAN, stretches) - 1
    chunks = groups // chunk
    bits = groups.bit_length() - 1
    stretch = lax.axis_index("stretch")
    me = lax.axis_index("seq")
    head = lax.rem(me, HEADS)
    share = me // HEADS

    def cols(index):
        return pl.ds(pl.multiple_of(index * HD, HD), HD)

    w_copy = pltpu.make_async_copy(w_ref, w_s, load_sem.at[0])
    tok_copy = pltpu.make_async_copy(tok_ref, tok_s, load_sem.at[1])
    own = [
        pltpu.make_async_copy(q_ref.at[:, cols(head)], qbuf.at[head], local_sem.at[0]),
        pltpu.make_async_copy(k_ref.at[:, cols(head)], kbuf.at[me], local_sem.at[1]),
        pltpu.make_async_copy(v_ref.at[:, cols(head)], vbuf.at[me], local_sem.at[2]),
    ]

    barrier = pltpu.get_barrier_semaphore()

    for bit in range(bits):
        pl.semaphore_signal(barrier, inc=1, device_id=(stretch, flip(me, 1 << bit)), device_id_type=MESH)
    for dist in range(1, prior + 1):
        @pl.when(stretch + dist < stretches)
        def _():
            pl.semaphore_signal(barrier, inc=1, device_id=(stretch + dist, me), device_id_type=MESH)

        @pl.when(stretch >= dist)
        def _():
            pl.semaphore_signal(barrier, inc=1, device_id=(stretch - dist, me), device_id_type=MESH)

    for copy in own:
        copy.start()
    w_copy.start()
    tok_copy.start()
    partners = jnp.minimum(stretch, prior) + jnp.minimum(stretches - 1 - stretch, prior)
    pl.semaphore_wait(barrier, bits + partners)

    def q_copy(mask):
        peer = flip(me, mask)
        return pltpu.make_async_remote_copy(
            src_ref=q_ref.at[:, cols(lax.rem(peer, HEADS))], dst_ref=qbuf.at[head],
            send_sem=q_send.at[mask], recv_sem=q_recv.at[head],
            device_id=(stretch, peer), device_id_type=MESH)

    def kv_copy(mask, which):
        peer = flip(me, mask)
        src, dst, recv = ((k_ref, kbuf, k_recv), (v_ref, vbuf, v_recv))[which]
        return pltpu.make_async_remote_copy(
            src_ref=src.at[:, cols(lax.rem(peer, HEADS))], dst_ref=dst.at[me],
            send_sem=kv_send.at[which, mask], recv_sem=recv.at[me],
            device_id=(stretch, peer), device_id_type=MESH)

    for turn, masks in enumerate(rounds_of(bits)):
        if turn:
            near = flip(me, 1 << (turn - 1))
            pl.semaphore_signal(ready.at[turn - 1], inc=1, device_id=(stretch, near), device_id_type=MESH)
            pl.semaphore_wait(ready.at[turn - 1], 1)
        for mask in masks:
            if mask < HEADS:
                q_copy(mask).start()
            kv_copy(mask, 0).start()
            kv_copy(mask, 1).start()

    top_s[...] = jnp.full_like(top_s, -1e30)
    sum_s[...] = jnp.zeros_like(sum_s)
    acc_s[...] = jnp.zeros_like(acc_s)

    for copy in own:
        copy.wait()

    def arrived(buf, sems, slot, sends):
        return pltpu.make_async_remote_copy(
            src_ref=buf.at[slot], dst_ref=buf.at[slot], send_sem=sends, recv_sem=sems.at[slot],
            device_id=(stretch, lax.rem(me + 1, groups)), device_id_type=MESH)

    @pl.loop(1, HEADS)
    def _(off):
        arrived(qbuf, q_recv, lax.rem(head + off, HEADS), q_send.at[0]).wait_recv()

    factor = math.log2(math.e) / math.sqrt(HD)
    keys_each = chunk * count
    per = math.gcd(HEADS, 4)
    rows = per * count

    def absorb_block(block, key_ref, value_ref):
        key_block = key_ref[...].reshape(keys_each, HD)
        value_block = value_ref[...].reshape(keys_each, HD)
        span = pl.ds(pl.multiple_of(block * rows, rows), rows)
        query = qbuf[pl.ds(block * per, per)].reshape(rows, HD)
        scores = lax.dot_general(query, key_block, (((1,), (1,)), ((), ())),
                                 preferred_element_type=jnp.float32)
        old = top_s[span, :]
        new = jnp.maximum(old, jnp.max(scores, axis=1, keepdims=True))
        top_s[span, :] = new
        fade = jnp.exp2((old - new) * factor)
        weights = [
            jnp.exp2((scores[:, part * HD:(part + 1) * HD] - new) * factor)
            for part in range(keys_each // HD)
        ]
        sum_s[span, :] = sum_s[span, :] * fade + functools.reduce(jnp.add, weights)
        expo = jnp.concatenate([part.astype(jnp.bfloat16) for part in weights], axis=1)
        acc_s[span, :] = acc_s[span, :] * fade + jnp.dot(
            expo, value_block, preferred_element_type=jnp.float32)

    def absorb(key_ref, value_ref):
        for block in range(HEADS // per):
            absorb_block(block, key_ref, value_ref)

    def forward(first, slot, dist, which):
        src, dst, recv = ((kbuf, kprior, kp_recv), (vbuf, vprior, vp_recv))[which]
        return pltpu.make_async_remote_copy(
            src_ref=src.at[pl.ds(first, chunk)], dst_ref=dst.at[dist - 1, pl.ds(first, chunk)],
            send_sem=fwd_send.at[which, dist - 1, slot], recv_sem=recv.at[dist - 1, slot],
            device_id=(stretch + dist, me), device_id_type=MESH)

    my_chunk = lax.div(me, chunk)

    def chunk_at(index):
        slot = 0
        for bit in range(chunks.bit_length() - 1):
            step = 1 << bit
            slot = slot + step * lax.rem(lax.div(my_chunk, step) + index // step, 2)
        return slot

    def take(index):
        slot = chunk_at(index)
        first = slot * chunk
        for step in range(chunk):
            source = first + step

            @pl.when(source != me)
            def _():
                arrived(kbuf, k_recv, source, kv_send.at[0, 0]).wait_recv()
                arrived(vbuf, v_recv, source, kv_send.at[0, 0]).wait_recv()

        for dist in range(1, prior + 1):
            @pl.when(stretch + dist < stretches)
            def _():
                forward(first, slot, dist, 0).start()
                forward(first, slot, dist, 1).start()
        return slot, pl.ds(first, chunk)

    def take_prior(dist, slot, part):
        for src, recv in ((kprior, kp_recv), (vprior, vp_recv)):
            pltpu.make_async_remote_copy(
                src_ref=src.at[dist - 1, part], dst_ref=src.at[dist - 1, part],
                send_sem=fwd_send.at[0, dist - 1, slot], recv_sem=recv.at[dist - 1, slot],
                device_id=(stretch - dist, me), device_id_type=MESH).wait_recv()

    @pl.loop(0, chunks - 1)
    def _(index):
        slot, part = take(index)
        absorb(kbuf.at[part], vbuf.at[part])
        for dist in range(1, prior + 1):
            @pl.when(stretch >= dist)
            def _():
                take_prior(dist, slot, part)
                absorb(kprior.at[dist - 1, part], vprior.at[dist - 1, part])

    def o_copy(other, slot):
        return pltpu.make_async_remote_copy(
            src_ref=obuf.at[other], dst_ref=att.at[:, cols(head)],
            send_sem=o_send.at[slot], recv_sem=o_recv.at[head],
            device_id=(stretch, share * HEADS + other), device_id_type=MESH)

    own_out = pltpu.make_async_copy(obuf.at[head], att.at[:, cols(head)], local_sem.at[0])
    slot, part = take(chunks - 1)
    absorb(kbuf.at[part], vbuf.at[part])
    blocks = HEADS // per
    home = lax.div(head, per)
    sent = []
    for turn in range(blocks):
        block = lax.rem(home + 1 + turn, blocks)
        for dist in range(1, prior + 1):
            @pl.when(stretch >= dist)
            def _():
                if turn == 0:
                    take_prior(dist, slot, part)
                absorb_block(block, kprior.at[dist - 1, part], vprior.at[dist - 1, part])
        for step in range(per):
            source = block * per + step
            span = pl.ds(pl.multiple_of(source * count, count), count)
            total = jnp.sum(sum_s[span, :], axis=1, keepdims=True)
            obuf[source] = (acc_s[span, :] / total).astype(jnp.bfloat16)
        for step in range(per):
            other = block * per + flip(lax.rem(head, per), step)
            if turn == blocks - 1 and step == 0:
                own_out.start()
            else:
                copy = o_copy(other, turn * per + step)
                copy.start()
                sent.append(copy)

    w_copy.wait()
    tok_copy.wait()

    table = gate_ref[...]
    picked = lax.broadcasted_iota(jnp.int32, table.shape, 0) == step_ref[0]
    gate = jnp.sum(jnp.where(picked, table, 0.0), axis=0, keepdims=True)

    own_out.wait()

    @pl.loop(1, HEADS)
    def _(off):
        other = lax.rem(head + off, HEADS)
        pltpu.make_async_remote_copy(
            src_ref=obuf.at[other], dst_ref=att.at[:, cols(other)],
            send_sem=o_send.at[other], recv_sem=o_recv.at[other],
            device_id=(stretch, share * HEADS + other), device_id_type=MESH).wait_recv()

    proj = jnp.dot(att[...], w_s[...], preferred_element_type=jnp.float32)
    mean_sq = jnp.mean(proj * proj, axis=1, keepdims=True)
    normed = proj * lax.rsqrt(mean_sq + 1e-06)
    out_ref[...] = (tok_s[...].astype(jnp.float32) + gate * normed).astype(jnp.bfloat16)

    for copy in sent:
        copy.wait_send()
    for mask in range(1, groups):
        if mask < HEADS:
            q_copy(mask).wait_send()
        kv_copy(mask, 0).wait_send()
        kv_copy(mask, 1).wait_send()
    for dist in range(1, prior + 1):
        @pl.when(stretch + dist < stretches)
        def _():
            @pl.loop(0, chunks)
            def _(slot):
                forward(slot * chunk, slot, dist, 0).wait_send()
                forward(slot * chunk, slot, dist, 1).wait_send()


def solution(mesh):
    stretches, groups = mesh.shape["stretch"], mesh.shape["seq"]
    prior = max(1, min(SPAN, stretches) - 1)
    chunk = math.gcd(groups, 4)

    def on_device(queries, keys, values, tokens, out_weight, gate_table, timesteps):
        count = queries.shape[0]
        block = (count, HD)
        dma = pltpu.SemaphoreType.DMA
        anywhere = pl.BlockSpec(memory_space=pl.ANY)
        vmem = pl.BlockSpec(memory_space=pltpu.VMEM)
        rows = HEADS * count
        return pl.pallas_call(
            functools.partial(kernel, groups, stretches, chunk),
            out_shape=jax.ShapeDtypeStruct(tokens.shape, jnp.bfloat16),
            in_specs=[anywhere] * 5 + [vmem, pl.BlockSpec(memory_space=pltpu.SMEM)],
            out_specs=vmem,
            scratch_shapes=[
                pltpu.VMEM((HEADS, *block), jnp.bfloat16),
                pltpu.VMEM((groups, *block), jnp.bfloat16),
                pltpu.VMEM((groups, *block), jnp.bfloat16),
                pltpu.VMEM((prior, groups, *block), jnp.bfloat16),
                pltpu.VMEM((prior, groups, *block), jnp.bfloat16),
                pltpu.VMEM((rows, HD), jnp.float32),
                pltpu.VMEM((rows, HD), jnp.float32),
                pltpu.VMEM((rows, HD), jnp.float32),
                pltpu.VMEM((HEADS, *block), jnp.bfloat16),
                pltpu.VMEM((count, HEADS * HD), jnp.bfloat16),
                pltpu.VMEM(out_weight.shape, jnp.bfloat16),
                pltpu.VMEM(tokens.shape, jnp.bfloat16),
                dma((2,)),
                dma((3,)),
                dma((HEADS,)),
                dma((HEADS,)),
                dma((2, groups)),
                dma((groups,)),
                dma((groups,)),
                dma((2, prior, groups // chunk)),
                dma((prior, groups // chunk)),
                dma((prior, groups // chunk)),
                dma((HEADS,)),
                dma((HEADS,)),
                pltpu.SemaphoreType.REGULAR((max(1, groups.bit_length() - 1),)),
            ],
            compiler_params=pltpu.CompilerParams(collective_id=0, has_side_effects=True),
        )(queries, keys, values, tokens, out_weight, gate_table, timesteps)

    row = P(("stretch", "seq"), None)
    return jax.shard_map(
        on_device, mesh=mesh,
        in_specs=(row, row, row, row, P(), P(), P(("stretch", "seq"))),
        out_specs=row, check_vma=False)
```

```python
import functools
import math

import jax
import jax.numpy as jnp
from jax import lax
from jax.experimental import pallas as pl
from jax.experimental.pallas import tpu as pltpu
from jax.sharding import PartitionSpec as P

HD = 128
HEADS = 8
SPAN = 3
MESH = pl.DeviceIdType.MESH


def flip(base, mask):
    result = base
    for bit in range(mask.bit_length()):
        step = 1 << bit
        if mask & step:
            result = result + step * (1 - 2 * lax.rem(lax.div(base, step), 2))
    return result


def rounds_of(bits):
    known = {0} | {1 << bit for bit in range(bits)}
    rounds = [sorted(known - {0})]
    for bit in range(bits):
        fresh = {mask ^ (1 << bit) for mask in known} - known
        if not fresh:
            break
        rounds.append(sorted(fresh))
        known |= fresh
    return rounds


def kernel(groups, stretches, chunk, q_ref, k_ref, v_ref, tok_ref, w_ref, gate_ref, step_ref, out_ref,
           qbuf, kbuf, vbuf, kprior, vprior, top_s, sum_s, acc_s, obuf, att, w_s, tok_s,
           load_sem, local_sem, q_send, q_recv, kv_send, k_recv, v_recv,
           fwd_send, kp_recv, vp_recv, o_send, o_recv, ready):
    count = q_ref.shape[0]
    prior = min(SPAN, stretches) - 1
    chunks = groups // chunk
    bits = groups.bit_length() - 1
    stretch = lax.axis_index("stretch")
    me = lax.axis_index("seq")
    head = lax.rem(me, HEADS)
    share = me // HEADS

    def cols(index):
        return pl.ds(pl.multiple_of(index * HD, HD), HD)

    w_copy = pltpu.make_async_copy(w_ref, w_s, load_sem.at[0])
    tok_copy = pltpu.make_async_copy(tok_ref, tok_s, load_sem.at[1])
    own = [
        pltpu.make_async_copy(q_ref.at[:, cols(head)], qbuf.at[head], local_sem.at[0]),
        pltpu.make_async_copy(k_ref.at[:, cols(head)], kbuf.at[me], local_sem.at[1]),
        pltpu.make_async_copy(v_ref.at[:, cols(head)], vbuf.at[me], local_sem.at[2]),
    ]

    barrier = pltpu.get_barrier_semaphore()

    for bit in range(bits):
        pl.semaphore_signal(barrier, inc=1, device_id=(stretch, flip(me, 1 << bit)), device_id_type=MESH)
    for dist in range(1, prior + 1):
        @pl.when(stretch + dist < stretches)
        def _():
            pl.semaphore_signal(barrier, inc=1, device_id=(stretch + dist, me), device_id_type=MESH)

        @pl.when(stretch >= dist)
        def _():
            pl.semaphore_signal(barrier, inc=1, device_id=(stretch - dist, me), device_id_type=MESH)

    for copy in own:
        copy.start()
    w_copy.start()
    tok_copy.start()
    partners = jnp.minimum(stretch, prior) + jnp.minimum(stretches - 1 - stretch, prior)
    pl.semaphore_wait(barrier, bits + partners)

    def q_copy(mask):
        peer = flip(me, mask)
        return pltpu.make_async_remote_copy(
            src_ref=q_ref.at[:, cols(lax.rem(peer, HEADS))], dst_ref=qbuf.at[head],
            send_sem=q_send.at[mask], recv_sem=q_recv.at[head],
            device_id=(stretch, peer), device_id_type=MESH)

    def kv_copy(mask, which):
        peer = flip(me, mask)
        src, dst, recv = ((k_ref, kbuf, k_recv), (v_ref, vbuf, v_recv))[which]
        return pltpu.make_async_remote_copy(
            src_ref=src.at[:, cols(lax.rem(peer, HEADS))], dst_ref=dst.at[me],
            send_sem=kv_send.at[which, mask], recv_sem=recv.at[me],
            device_id=(stretch, peer), device_id_type=MESH)

    for turn, masks in enumerate(rounds_of(bits)):
        if turn:
            near = flip(me, 1 << (turn - 1))
            pl.semaphore_signal(ready.at[turn - 1], inc=1, device_id=(stretch, near), device_id_type=MESH)
            pl.semaphore_wait(ready.at[turn - 1], 1)
        for mask in masks:
            if mask < HEADS:
                q_copy(mask).start()
            kv_copy(mask, 0).start()
            kv_copy(mask, 1).start()

    top_s[...] = jnp.full_like(top_s, -1e30)
    sum_s[...] = jnp.zeros_like(sum_s)
    acc_s[...] = jnp.zeros_like(acc_s)

    for copy in own:
        copy.wait()

    def arrived(buf, sems, slot, sends):
        return pltpu.make_async_remote_copy(
            src_ref=buf.at[slot], dst_ref=buf.at[slot], send_sem=sends, recv_sem=sems.at[slot],
            device_id=(stretch, lax.rem(me + 1, groups)), device_id_type=MESH)

    @pl.loop(1, HEADS)
    def _(off):
        arrived(qbuf, q_recv, lax.rem(head + off, HEADS), q_send.at[0]).wait_recv()

    factor = math.log2(math.e) / math.sqrt(HD)
    keys_each = chunk * count
    per = math.gcd(HEADS, 4)
    rows = per * count

    def absorb_block(block, key_ref, value_ref):
        key_block = key_ref[...].reshape(keys_each, HD)
        value_block = value_ref[...].reshape(keys_each, HD)
        span = pl.ds(pl.multiple_of(block * rows, rows), rows)
        query = qbuf[pl.ds(block * per, per)].reshape(rows, HD)
        scores = lax.dot_general(query, key_block, (((1,), (1,)), ((), ())),
                                 preferred_element_type=jnp.float32)
        old = top_s[span, :]
        new = jnp.maximum(old, jnp.max(scores, axis=1, keepdims=True))
        top_s[span, :] = new
        fade = jnp.exp2((old - new) * factor)
        weights = [
            jnp.exp2((scores[:, part * HD:(part + 1) * HD] - new) * factor)
            for part in range(keys_each // HD)
        ]
        sum_s[span, :] = sum_s[span, :] * fade + functools.reduce(jnp.add, weights)
        expo = jnp.concatenate([part.astype(jnp.bfloat16) for part in weights], axis=1)
        acc_s[span, :] = acc_s[span, :] * fade + jnp.dot(
            expo, value_block, preferred_element_type=jnp.float32)

    def absorb(key_ref, value_ref):
        for block in range(HEADS // per):
            absorb_block(block, key_ref, value_ref)

    def forward(first, slot, dist, which):
        src, dst, recv = ((kbuf, kprior, kp_recv), (vbuf, vprior, vp_recv))[which]
        return pltpu.make_async_remote_copy(
            src_ref=src.at[pl.ds(first, chunk)], dst_ref=dst.at[dist - 1, pl.ds(first, chunk)],
            send_sem=fwd_send.at[which, dist - 1, slot], recv_sem=recv.at[dist - 1, slot],
            device_id=(stretch + dist, me), device_id_type=MESH)

    my_chunk = lax.div(me, chunk)

    def chunk_at(index):
        slot = 0
        for bit in range(chunks.bit_length() - 1):
            step = 1 << bit
            slot = slot + step * lax.rem(lax.div(my_chunk, step) + index // step, 2)
        return slot

    def take(index):
        slot = chunk_at(index)
        first = slot * chunk
        for step in range(chunk):
            source = first + step

            @pl.when(source != me)
            def _():
                arrived(kbuf, k_recv, source, kv_send.at[0, 0]).wait_recv()
                arrived(vbuf, v_recv, source, kv_send.at[0, 0]).wait_recv()

        for dist in range(1, prior + 1):
            @pl.when(stretch + dist < stretches)
            def _():
                forward(first, slot, dist, 0).start()
                forward(first, slot, dist, 1).start()
        return slot, pl.ds(first, chunk)

    def take_prior(dist, slot, part):
        for src, recv in ((kprior, kp_recv), (vprior, vp_recv)):
            pltpu.make_async_remote_copy(
                src_ref=src.at[dist - 1, part], dst_ref=src.at[dist - 1, part],
                send_sem=fwd_send.at[0, dist - 1, slot], recv_sem=recv.at[dist - 1, slot],
                device_id=(stretch - dist, me), device_id_type=MESH).wait_recv()

    @pl.loop(0, chunks - 1)
    def _(index):
        slot, part = take(index)
        absorb(kbuf.at[part], vbuf.at[part])
        for dist in range(1, prior + 1):
            @pl.when(stretch >= dist)
            def _():
                take_prior(dist, slot, part)
                absorb(kprior.at[dist - 1, part], vprior.at[dist - 1, part])

    def o_copy(other, slot):
        return pltpu.make_async_remote_copy(
            src_ref=obuf.at[other], dst_ref=att.at[:, cols(head)],
            send_sem=o_send.at[slot], recv_sem=o_recv.at[head],
            device_id=(stretch, share * HEADS + other), device_id_type=MESH)

    own_out = pltpu.make_async_copy(obuf.at[head], att.at[:, cols(head)], local_sem.at[0])
    slot, part = take(chunks - 1)
    absorb(kbuf.at[part], vbuf.at[part])
    blocks = HEADS // per
    home = lax.div(head, per)
    sent = []
    for turn in range(blocks):
        block = lax.rem(home + 1 + turn, blocks)
        for dist in range(1, prior + 1):
            @pl.when(stretch >= dist)
            def _():
                if turn == 0:
                    take_prior(dist, slot, part)
                absorb_block(block, kprior.at[dist - 1, part], vprior.at[dist - 1, part])
        for step in range(per):
            source = block * per + step
            span = pl.ds(pl.multiple_of(source * count, count), count)
            total = jnp.sum(sum_s[span, :], axis=1, keepdims=True)
            obuf[source] = (acc_s[span, :] / total).astype(jnp.bfloat16)
        for step in range(per):
            other = block * per + flip(lax.rem(head, per), step)
            if turn == blocks - 1 and step == 0:
                own_out.start()
            else:
                copy = o_copy(other, turn * per + step)
                copy.start()
                sent.append(copy)

    w_copy.wait()
    tok_copy.wait()

    table = gate_ref[...]
    picked = lax.broadcasted_iota(jnp.int32, table.shape, 0) == step_ref[0]
    gate = jnp.sum(jnp.where(picked, table, 0.0), axis=0, keepdims=True)

    own_out.wait()
    for step in range(HEADS):
        mask = step
        if mask:
            other = flip(head, mask)
            pltpu.make_async_remote_copy(
                src_ref=obuf.at[other], dst_ref=att.at[:, cols(other)],
                send_sem=o_send.at[0], recv_sem=o_recv.at[other],
                device_id=(stretch, share * HEADS + other), device_id_type=MESH).wait_recv()
        if step % per == per - 1:
            wide = per * HD
            base = pl.multiple_of(lax.div(flip(head, step), per) * wide, wide)
            term = jnp.dot(att[:, pl.ds(base, wide)], w_s[pl.ds(base, wide), :],
                           preferred_element_type=jnp.float32)
            proj = term if step < per else proj + term
    mean_sq = jnp.mean(proj * proj, axis=1, keepdims=True)
    normed = proj * lax.rsqrt(mean_sq + 1e-06)
    out_ref[...] = (tok_s[...].astype(jnp.float32) + gate * normed).astype(jnp.bfloat16)

    for copy in sent:
        copy.wait_send()
    for mask in range(1, groups):
        if mask < HEADS:
            q_copy(mask).wait_send()
        kv_copy(mask, 0).wait_send()
        kv_copy(mask, 1).wait_send()
    for dist in range(1, prior + 1):
        @pl.when(stretch + dist < stretches)
        def _():
            @pl.loop(0, chunks)
            def _(slot):
                forward(slot * chunk, slot, dist, 0).wait_send()
                forward(slot * chunk, slot, dist, 1).wait_send()


def solution(mesh):
    stretches, groups = mesh.shape["stretch"], mesh.shape["seq"]
    prior = max(1, min(SPAN, stretches) - 1)
    chunk = math.gcd(groups, 4)

    def on_device(queries, keys, values, tokens, out_weight, gate_table, timesteps):
        count = queries.shape[0]
        block = (count, HD)
        dma = pltpu.SemaphoreType.DMA
        anywhere = pl.BlockSpec(memory_space=pl.ANY)
        vmem = pl.BlockSpec(memory_space=pltpu.VMEM)
        rows = HEADS * count
        return pl.pallas_call(
            functools.partial(kernel, groups, stretches, chunk),
            out_shape=jax.ShapeDtypeStruct(tokens.shape, jnp.bfloat16),
            in_specs=[anywhere] * 5 + [vmem, pl.BlockSpec(memory_space=pltpu.SMEM)],
            out_specs=vmem,
            scratch_shapes=[
                pltpu.VMEM((HEADS, *block), jnp.bfloat16),
                pltpu.VMEM((groups, *block), jnp.bfloat16),
                pltpu.VMEM((groups, *block), jnp.bfloat16),
                pltpu.VMEM((prior, groups, *block), jnp.bfloat16),
                pltpu.VMEM((prior, groups, *block), jnp.bfloat16),
                pltpu.VMEM((rows, HD), jnp.float32),
                pltpu.VMEM((rows, HD), jnp.float32),
                pltpu.VMEM((rows, HD), jnp.float32),
                pltpu.VMEM((HEADS, *block), jnp.bfloat16),
                pltpu.VMEM((count, HEADS * HD), jnp.bfloat16),
                pltpu.VMEM(out_weight.shape, jnp.bfloat16),
                pltpu.VMEM(tokens.shape, jnp.bfloat16),
                dma((2,)),
                dma((3,)),
                dma((HEADS,)),
                dma((HEADS,)),
                dma((2, groups)),
                dma((groups,)),
                dma((groups,)),
                dma((2, prior, groups // chunk)),
                dma((prior, groups // chunk)),
                dma((prior, groups // chunk)),
                dma((HEADS,)),
                dma((HEADS,)),
                pltpu.SemaphoreType.REGULAR((max(1, groups.bit_length() - 1),)),
            ],
            compiler_params=pltpu.CompilerParams(collective_id=0, has_side_effects=True),
        )(queries, keys, values, tokens, out_weight, gate_table, timesteps)

    row = P(("stretch", "seq"), None)
    return jax.shard_map(
        on_device, mesh=mesh,
        in_specs=(row, row, row, row, P(), P(), P(("stretch", "seq"))),
        out_specs=row, check_vma=False)
```
